256 devices in a mesh: blk: 16 (over y, x_hi, core), uly: 16 (over z, x_lo).
Axes of the slice: x: 4 (x_hi: 2, x_lo: 2; x = x_hi * 2 + x_lo), y: 4, z: 8, core: 2. Of those that a mesh axis runs over, the one named last changes fastest.
Arguments:
- queries: bfloat16 [65536, 4096], P(('blk', 'uly')), may hold values from -6 to 6
- keys: bfloat16 [65536, 4096], P(('blk', 'uly')), may hold values from -6 to 6
- values: bfloat16 [65536, 4096], P(('blk', 'uly')), may hold values from -6 to 6
- doc_start: int32 [65536], P('blk'), may hold values from 0 to 65535, as said below
Outputs:
- attended: bfloat16 [65536, 4096], P(('blk', 'uly'))
The draws below stay inside these ranges and needn't reach their ends.
Inputs may be any that keep to these rules, and one draw needn't show every extreme that they name: doc_start[0] = 0, and for t > 0 doc_start[t] is either t or doc_start[t - 1].
All inputs are finite; a program needn't handle non-finite values.
Results may differ from the reference program's by a relative error of at most 0.0026.
Values may be sent and summed in bfloat16 or wider, within the bound.
A program may use at most 128 MiB of HBM per device.

```python
import math
import jax
import jax.numpy as jnp
from jax import lax

HEADS = 32
HEAD_DIM = 128
TOKENS = 65536
WINDOW = 2048
QBLOCK = 512


def doc_starts(key):
    base_key = jax.random.fold_in(key, 7)
    region_len = WINDOW // 2
    position = jnp.arange(TOKENS, dtype=jnp.int32)
    region = position // region_len
    top_power = int(math.log2(2 * WINDOW))
    powers = jax.random.randint(jax.random.fold_in(base_key, 1), (TOKENS // region_len + 1,), 3, top_power + 1)
    spans = (2 ** powers).astype(jnp.int32)
    rolls = jax.random.randint(jax.random.fold_in(base_key, 2), (TOKENS,), 0, spans[region])
    marked = (rolls == 0) | (position == 0) | (position == TOKENS - 1)
    return lax.cummax(jnp.where(marked, position, 0), axis=0)


def base_field(key):
    width = HEADS * HEAD_DIM
    return jnp.clip(jax.random.normal(key, (TOKENS, width), jnp.float32), -6.0, 6.0)


def draw_doc_start(key, part):
    return doc_starts(key)


def draw_queries(key, part):
    field = base_field(jax.random.fold_in(key, 11))
    return field.astype(jnp.bfloat16)


def draw_keys(key, part):
    field = base_field(jax.random.fold_in(key, 12))
    return field.astype(jnp.bfloat16)


def level_of(key, extent, shards, smallest, high):
    factor_of = 1.0
    for axis_at, blocks in shards:
        heights = jax.random.uniform(jax.random.fold_in(jax.random.fold_in(key, 6), axis_at), (blocks,), jnp.float32, smallest / len(shards), high / len(shards))
        factor_of = factor_of * jnp.repeat(jnp.exp(heights), extent[axis_at] // blocks).reshape((-1,) + (1,) * (len(extent) - 1 - axis_at))
    return factor_of


def noise(key, extent, deviation, bound, split=(), kind=jnp.bfloat16):
    values = deviation * jax.random.normal(key, extent, jnp.float32)
    if split:
        values = values * level_of(key, extent, split, -0.22, 0.18)
    return jnp.clip(values, -bound, bound).astype(kind)


def setup_inputs(seed: int = 0) -> dict:
    arg_keys = jax.random.split(jax.random.key(seed), 5)
    queries = draw_queries(jax.random.fold_in(arg_keys[4], 71), 0)
    keys = draw_keys(jax.random.fold_in(arg_keys[4], 71), 0)
    values = noise(arg_keys[2], (TOKENS, HEADS * HEAD_DIM), 1.0, 6.0, ((0, 256),))
    doc_start = draw_doc_start(jax.random.fold_in(arg_keys[4], 71), 0)
    return dict(queries=queries, keys=keys, values=values, doc_start=doc_start)


def reference(queries, keys, values, doc_start):
    total = queries.shape[0]
    width = HEADS * HEAD_DIM
    query_all = queries.reshape(total, HEADS, HEAD_DIM)
    padding = jnp.zeros((WINDOW, width), keys.dtype)
    keys_wide = jnp.concatenate([padding, keys], axis=0).reshape(total + WINDOW, HEADS, HEAD_DIM)
    values_wide = jnp.concatenate([padding, values], axis=0).reshape(total + WINDOW, HEADS, HEAD_DIM)
    score_scale = 1.0 / math.sqrt(HEAD_DIM)

    def attend_block(block_index):
        first = (block_index * QBLOCK).astype(jnp.int32)
        query_rows = lax.dynamic_slice_in_dim(query_all, first, QBLOCK, 0).astype(jnp.float32)
        key_rows = lax.dynamic_slice_in_dim(keys_wide, first, QBLOCK + WINDOW, 0).astype(jnp.float32)
        value_rows = lax.dynamic_slice_in_dim(values_wide, first, QBLOCK + WINDOW, 0).astype(jnp.float32)
        starts = lax.dynamic_slice_in_dim(doc_start, first, QBLOCK, 0)
        query_pos = first + jnp.arange(QBLOCK, dtype=jnp.int32)
        key_pos = first - WINDOW + jnp.arange(QBLOCK + WINDOW, dtype=jnp.int32)
        allowed = (key_pos[None, :] <= query_pos[:, None]) & (key_pos[None, :] > query_pos[:, None] - WINDOW) & (key_pos[None, :] >= starts[:, None])
        scores = jnp.einsum('qhd,khd->hqk', query_rows, key_rows) * score_scale
        scores = jnp.where(allowed[None], scores, -jnp.inf)
        row_max = lax.optimization_barrier(jnp.max(scores, axis=-1, keepdims=True))
        probs = jnp.exp(scores - row_max)
        totals = lax.optimization_barrier(jnp.sum(probs, axis=-1))
        weights = probs.astype(jnp.bfloat16)
        mixed = jnp.einsum('hqk,khd->qhd', weights.astype(jnp.float32), value_rows)
        mixed = mixed / jnp.transpose(totals)[:, :, None]
        return mixed.astype(jnp.bfloat16).reshape(QBLOCK, width)
    blocks = lax.map(attend_block, jnp.arange(total // QBLOCK, dtype=jnp.int32))
    return blocks.reshape(total, width)
```

```python
import functools
import math

import jax
import jax.numpy as jnp
from jax import lax
from jax.experimental import pallas as pl
from jax.experimental.pallas import tpu as pltpu
from jax.sharding import PartitionSpec as P

HEAD_DIM = 128
LANES = 128
MESH = pl.DeviceIdType.MESH
LAST_DIMS = (((1,), (1,)), ((), ()))
SCALE = math.log2(math.e) / math.sqrt(HEAD_DIM)
Q, K, V = 0, 1, 2


def kernel(
    peers, stretches, rows, heads,
    queries, keys, values, doc_start, attended,
    q_buf, k_buf, v_buf, o_buf, oldest, scores,
    in_send, in_recv, halo_send, halo_recv, out_send, out_recv,
):
    stretch = peers * rows
    window = stretch // 2
    span = window + rows
    blk, me = lax.axis_index("blk"), lax.axis_index("uly")
    after, before = lax.rem(blk + 1, stretches), lax.rem(blk + stretches - 1, stretches)

    def peer(i):
        half = (i + 1) // 2
        return lax.rem(me + jnp.where(i % 2 == 1, half, peers - half), peers)

    def token_rows(p, shift=0):
        return pl.ds(pl.multiple_of(p * rows + shift, rows), rows)

    def head_columns(p, head):
        return pl.ds(pl.multiple_of((p * heads + head) * HEAD_DIM, HEAD_DIM), HEAD_DIM)

    barrier = pltpu.get_barrier_semaphore()

    def greet(i, carry):
        pl.semaphore_signal(barrier, inc=1, device_id=(blk, peer(i)), device_id_type=MESH)
        return carry

    lax.fori_loop(1, peers, greet, 0)
    pl.semaphore_signal(barrier, inc=1, device_id=(before, me), device_id_type=MESH)
    pl.semaphore_wait(barrier, peers)

    operands = {Q: (queries, q_buf, 0), K: (keys, k_buf, window), V: (values, v_buf, window)}
    order = (K, V, Q)

    def inbound(head, t, src_peer, dst_peer):
        source, buffer, shift = operands[t]
        return pltpu.make_async_remote_copy(
            src_ref=source.at[:, head_columns(dst_peer, head)],
            dst_ref=buffer.at[head, token_rows(src_peer, shift)],
            send_sem=in_send.at[head, t, dst_peer],
            recv_sem=in_recv.at[head, t, src_peer],
            device_id=(blk, dst_peer),
            device_id_type=MESH,
        )

    def own(head, t):
        source, buffer, shift = operands[t]
        return pltpu.make_async_copy(
            source.at[:, head_columns(me, head)],
            buffer.at[head, token_rows(me, shift)],
            in_recv.at[head, t, me],
        )

    for head in range(heads):
        for t in order:
            own(head, t).start()

            def send(i, carry):
                p = peer(i)
                inbound(head, t, me, p).start()
                return carry

            lax.fori_loop(1, peers, send, 0)

    for group in range(stretch // LANES):
        starts = jnp.transpose(jnp.broadcast_to(doc_start[group : group + 1, :], (LANES, LANES)))
        token = group * LANES + lax.broadcasted_iota(jnp.int32, (LANES, LANES), 0)
        oldest[group * LANES : (group + 1) * LANES, :] = jnp.maximum(
            starts - blk * stretch + window, token + 1
        )

    def arrived(head, t, low, high):
        def wait(p, carry):
            inbound(head, t, p, me).wait_recv()
            return carry

        lax.fori_loop(low, high, wait, 0)

    def halo(head, t):
        buffer = operands[t][1]
        return pltpu.make_async_remote_copy(
            src_ref=buffer.at[head, pl.ds(stretch, window)],
            dst_ref=buffer.at[head, pl.ds(0, window)],
            send_sem=halo_send.at[head, t],
            recv_sem=halo_recv.at[head, t],
            device_id=(after, me),
            device_id_type=MESH,
        )

    def outbound(head, src_peer, dst_peer):
        return pltpu.make_async_remote_copy(
            src_ref=o_buf.at[head, token_rows(dst_peer)],
            dst_ref=attended.at[:, head_columns(src_peer, head)],
            send_sem=out_send.at[head, dst_peer],
            recv_sem=out_recv.at[head, src_peer],
            device_id=(blk, dst_peer),
            device_id_type=MESH,
        )

    def own_out(head):
        return pltpu.make_async_copy(
            o_buf.at[head, token_rows(me)],
            attended.at[:, head_columns(me, head)],
            out_recv.at[head, me],
        )

    def send_out(head, p):
        @pl.when(p == me)
        def _():
            own_out(head).start()

        @pl.when(p != me)
        def _():
            outbound(head, me, p).start()

    def attend(head, p):
        first = p * rows

        def key_rows(c):
            return pl.ds(pl.multiple_of(first + c * rows, rows), rows)

        query = q_buf[head, token_rows(p)]
        low = oldest[token_rows(p)] - first
        lane = lax.broadcasted_iota(jnp.int32, (rows, LANES), 1)
        row = lax.broadcasted_iota(jnp.int32, (rows, LANES), 0)
        top = jnp.full((rows, LANES), -jnp.inf, jnp.float32)
        for c in range(span // rows):
            tile = lax.dot_general(
                query, k_buf[head, key_rows(c)], LAST_DIMS, preferred_element_type=jnp.float32
            )
            for at in range(c * rows, (c + 1) * rows, LANES):
                allowed = lane + at >= low
                if at >= window:
                    allowed = allowed & (lane <= row - (at - window))
                part = jnp.where(allowed, tile[:, at - c * rows : at - c * rows + LANES], -jnp.inf)
                top = jnp.maximum(top, part)
                scores[:, at : at + LANES] = part
        row_max = jnp.broadcast_to(jnp.max(top, axis=1, keepdims=True) * SCALE, (rows, LANES))
        mixed = jnp.zeros((rows, HEAD_DIM), jnp.float32)
        total = jnp.zeros((rows, LANES), jnp.float32)
        for c in range(span // rows):
            weights = []
            for at in range(c * rows, (c + 1) * rows, LANES):
                probs = jnp.exp2(scores[:, at : at + LANES] * SCALE - row_max)
                total = total + probs
                weights.append(probs.astype(jnp.bfloat16))
            mixed = mixed + jnp.dot(
                jnp.concatenate(weights, axis=1),
                v_buf[head, key_rows(c)],
                preferred_element_type=jnp.float32,
            )
        mixed = mixed / jnp.sum(total, axis=1, keepdims=True)
        o_buf[head, token_rows(p)] = mixed.astype(jnp.bfloat16)

    middle = peers // 2
    for head in range(heads):
        for t in (K, V):
            arrived(head, t, middle, peers)
            halo(head, t).start()
        for t in (K, V):
            arrived(head, t, 0, middle)
        arrived(head, Q, 0, peers)

        def block(p, carry):
            attend(head, p)
            send_out(head, p)
            return carry

        lax.fori_loop(middle, peers, block, 0)
        for t in (K, V):
            halo(head, t).wait_recv()
        lax.fori_loop(0, middle, block, 0)

    for head in range(heads):
        for t in (K, V):
            halo(head, t).wait_send()

        def settle(i, carry):
            p = peer(i)
            for t in order:
                inbound(head, t, me, p).wait_send()
            outbound(head, p, p).wait_recv()
            outbound(head, me, p).wait_send()
            return carry

        lax.fori_loop(1, peers, settle, 0)
        own_out(head).wait()


def shards(peers, stretches, queries, keys, values, doc_start):
    rows, width = queries.shape
    stretch = rows * peers
    window = stretch // 2
    heads = width // peers // HEAD_DIM
    anywhere = pl.BlockSpec(memory_space=pl.ANY)
    return pl.pallas_call(
        functools.partial(kernel, peers, stretches, rows, heads),
        out_shape=jax.ShapeDtypeStruct((rows, width), jnp.bfloat16),
        in_specs=[anywhere, anywhere, anywhere, pl.BlockSpec(memory_space=pltpu.VMEM)],
        out_specs=anywhere,
        scratch_shapes=[
            pltpu.VMEM((heads, stretch, HEAD_DIM), jnp.bfloat16),
            pltpu.VMEM((heads, stretch + window, HEAD_DIM), jnp.bfloat16),
            pltpu.VMEM((heads, stretch + window, HEAD_DIM), jnp.bfloat16),
            pltpu.VMEM((heads, stretch, HEAD_DIM), jnp.bfloat16),
            pltpu.VMEM((stretch, LANES), jnp.int32),
            pltpu.VMEM((rows, window + rows), jnp.float32),
            pltpu.SemaphoreType.DMA((heads, 3, peers)),
            pltpu.SemaphoreType.DMA((heads, 3, peers)),
            pltpu.SemaphoreType.DMA((heads, 3)),
            pltpu.SemaphoreType.DMA((heads, 3)),
            pltpu.SemaphoreType.DMA((heads, peers)),
            pltpu.SemaphoreType.DMA((heads, peers)),
        ],
        compiler_params=pltpu.CompilerParams(
            collective_id=0, has_side_effects=True, vmem_limit_bytes=48 << 20
        ),
    )(queries, keys, values, doc_start.reshape(stretch // LANES, LANES))


def solution(mesh):
    rows = P(("blk", "uly"), None)
    return jax.shard_map(
        functools.partial(shards, mesh.shape["uly"], mesh.shape["blk"]),
        mesh=mesh,
        in_specs=(rows, rows, rows, P("blk")),
        out_specs=rows,
        check_vma=False,
    )
```

```python
import functools
import math

import jax
import jax.numpy as jnp
from jax import lax
from jax.experimental import pallas as pl
from jax.experimental.pallas import tpu as pltpu
from jax.sharding import PartitionSpec as P

HEAD_DIM = 128
LANES = 128
MESH = pl.DeviceIdType.MESH
LAST_DIMS = (((1,), (1,)), ((), ()))
SCALE = math.log2(math.e) / math.sqrt(HEAD_DIM)
Q, K, V = 0, 1, 2


def kernel(
    peers, stretches, rows, heads,
    queries, keys, values, doc_start, attended,
    q_buf, k_buf, v_buf, o_buf, doc_buf, oldest, scores, doc_sem,
    in_send, in_recv, halo_send, halo_recv, out_send, out_recv,
):
    stretch = peers * rows
    window = stretch // 2
    span = window + rows
    blk, me = lax.axis_index("blk"), lax.axis_index("uly")
    after, before = lax.rem(blk + 1, stretches), lax.rem(blk + stretches - 1, stretches)

    def peer(i):
        half = (i + 1) // 2
        return lax.rem(me + jnp.where(i % 2 == 1, half, peers - half), peers)

    def token_rows(p, shift=0):
        return pl.ds(pl.multiple_of(p * rows + shift, rows), rows)

    def head_columns(p, head):
        return pl.ds(pl.multiple_of((p * heads + head) * HEAD_DIM, HEAD_DIM), HEAD_DIM)

    fetch = pltpu.make_async_copy(doc_start, doc_buf, doc_sem)
    fetch.start()
    barrier = pltpu.get_barrier_semaphore()

    def greet(i, carry):
        pl.semaphore_signal(barrier, inc=1, device_id=(blk, peer(i)), device_id_type=MESH)
        return carry

    lax.fori_loop(1, peers, greet, 0)
    pl.semaphore_signal(barrier, inc=1, device_id=(before, me), device_id_type=MESH)
    pl.semaphore_wait(barrier, peers)

    operands = {Q: (queries, q_buf, 0), K: (keys, k_buf, window), V: (values, v_buf, window)}
    order = (K, V, Q)

    def inbound(head, t, src_peer, dst_peer):
        source, buffer, shift = operands[t]
        return pltpu.make_async_remote_copy(
            src_ref=source.at[:, head_columns(dst_peer, head)],
            dst_ref=buffer.at[head, token_rows(src_peer, shift)],
            send_sem=in_send.at[head, t, dst_peer],
            recv_sem=in_recv.at[head, t, src_peer],
            device_id=(blk, dst_peer),
            device_id_type=MESH,
        )

    def own(head, t):
        source, buffer, shift = operands[t]
        return pltpu.make_async_copy(
            source.at[:, head_columns(me, head)],
            buffer.at[head, token_rows(me, shift)],
            in_recv.at[head, t, me],
        )

    for head in range(heads):
        for t in order:
            own(head, t).start()

            def send(i, carry):
                p = peer(i)
                inbound(head, t, me, p).start()
                return carry

            lax.fori_loop(1, peers, send, 0)

    fetch.wait()
    for group in range(stretch // LANES):
        starts = jnp.transpose(jnp.broadcast_to(doc_buf[group : group + 1, :], (LANES, LANES)))
        token = group * LANES + lax.broadcasted_iota(jnp.int32, (LANES, LANES), 0)
        oldest[group * LANES : (group + 1) * LANES, :] = jnp.maximum(
            starts - blk * stretch + window, token + 1
        )

    def arrived(head, t, low, high):
        def wait(p, carry):
            inbound(head, t, p, me).wait_recv()
            return carry

        lax.fori_loop(low, high, wait, 0)

    def halo(head, t):
        buffer = operands[t][1]
        return pltpu.make_async_remote_copy(
            src_ref=buffer.at[head, pl.ds(stretch, window)],
            dst_ref=buffer.at[head, pl.ds(0, window)],
            send_sem=halo_send.at[head, t],
            recv_sem=halo_recv.at[head, t],
            device_id=(after, me),
            device_id_type=MESH,
        )

    def outbound(head, src_peer, dst_peer):
        return pltpu.make_async_remote_copy(
            src_ref=o_buf.at[head, token_rows(dst_peer)],
            dst_ref=attended.at[:, head_columns(src_peer, head)],
            send_sem=out_send.at[head, dst_peer],
            recv_sem=out_recv.at[head, src_peer],
            device_id=(blk, dst_peer),
            device_id_type=MESH,
        )

    def own_out(head):
        return pltpu.make_async_copy(
            o_buf.at[head, token_rows(me)],
            attended.at[:, head_columns(me, head)],
            out_recv.at[head, me],
        )

    def send_out(head, p):
        @pl.when(p == me)
        def _():
            own_out(head).start()

        @pl.when(p != me)
        def _():
            outbound(head, me, p).start()

    def attend(head, p):
        first = p * rows

        def key_rows(c):
            return pl.ds(pl.multiple_of(first + c * rows, rows), rows)

        query = q_buf[head, token_rows(p)]
        low = oldest[token_rows(p)] - first
        lane = lax.broadcasted_iota(jnp.int32, (rows, LANES), 1)
        row = lax.broadcasted_iota(jnp.int32, (rows, LANES), 0)
        top = jnp.full((rows, LANES), -jnp.inf, jnp.float32)
        for c in range(span // rows):
            tile = lax.dot_general(
                query, k_buf[head, key_rows(c)], LAST_DIMS, preferred_element_type=jnp.float32
            )
            for at in range(c * rows, (c + 1) * rows, LANES):
                allowed = lane + at >= low
                if at >= window:
                    allowed = allowed & (lane <= row - (at - window))
                part = jnp.where(allowed, tile[:, at - c * rows : at - c * rows + LANES], -jnp.inf)
                top = jnp.maximum(top, part)
                scores[:, at : at + LANES] = part
        row_max = jnp.broadcast_to(jnp.max(top, axis=1, keepdims=True) * SCALE, (rows, LANES))
        mixed = jnp.zeros((rows, HEAD_DIM), jnp.float32)
        total = jnp.zeros((rows, LANES), jnp.float32)
        for c in range(span // rows):
            weights = []
            for at in range(c * rows, (c + 1) * rows, LANES):
                probs = jnp.exp2(scores[:, at : at + LANES] * SCALE - row_max)
                total = total + probs
                weights.append(probs.astype(jnp.bfloat16))
            mixed = mixed + jnp.dot(
                jnp.concatenate(weights, axis=1),
                v_buf[head, key_rows(c)],
                preferred_element_type=jnp.float32,
            )
        mixed = mixed / jnp.sum(total, axis=1, keepdims=True)
        o_buf[head, token_rows(p)] = mixed.astype(jnp.bfloat16)

    middle = peers // 2
    for head in range(heads):
        for t in (K, V):
            arrived(head, t, middle, peers)
            halo(head, t).start()
        for t in (K, V):
            arrived(head, t, 0, middle)
        arrived(head, Q, 0, peers)

        def block(p, carry):
            attend(head, p)
            send_out(head, p)
            return carry

        lax.fori_loop(middle, peers, block, 0)
        for t in (K, V):
            halo(head, t).wait_recv()
        lax.fori_loop(0, middle, block, 0)

    for head in range(heads):
        for t in (K, V):
            halo(head, t).wait_send()

        def settle(i, carry):
            p = peer(i)
            for t in order:
                inbound(head, t, me, p).wait_send()
            outbound(head, p, p).wait_recv()
            outbound(head, me, p).wait_send()
            return carry

        lax.fori_loop(1, peers, settle, 0)
        own_out(head).wait()


def shards(peers, stretches, queries, keys, values, doc_start):
    rows, width = queries.shape
    stretch = rows * peers
    window = stretch // 2
    heads = width // peers // HEAD_DIM
    anywhere = pl.BlockSpec(memory_space=pl.ANY)
    return pl.pallas_call(
        functools.partial(kernel, peers, stretches, rows, heads),
        out_shape=jax.ShapeDtypeStruct((rows, width), jnp.bfloat16),
        in_specs=[pl.BlockSpec(memory_space=pltpu.HBM)] * 4,
        out_specs=anywhere,
        scratch_shapes=[
            pltpu.VMEM((heads, stretch, HEAD_DIM), jnp.bfloat16),
            pltpu.VMEM((heads, stretch + window, HEAD_DIM), jnp.bfloat16),
            pltpu.VMEM((heads, stretch + window, HEAD_DIM), jnp.bfloat16),
            pltpu.VMEM((heads, stretch, HEAD_DIM), jnp.bfloat16),
            pltpu.VMEM((stretch // LANES, LANES), jnp.int32),
            pltpu.VMEM((stretch, LANES), jnp.int32),
            pltpu.VMEM((rows, window + rows), jnp.float32),
            pltpu.SemaphoreType.DMA,
            pltpu.SemaphoreType.DMA((heads, 3, peers)),
            pltpu.SemaphoreType.DMA((heads, 3, peers)),
            pltpu.SemaphoreType.DMA((heads, 3)),
            pltpu.SemaphoreType.DMA((heads, 3)),
            pltpu.SemaphoreType.DMA((heads, peers)),
            pltpu.SemaphoreType.DMA((heads, peers)),
        ],
        compiler_params=pltpu.CompilerParams(
            collective_id=0, has_side_effects=True, vmem_limit_bytes=48 << 20
        ),
    )(*(pltpu.with_memory_space_constraint(a, pltpu.HBM) for a in (queries, keys, values, doc_start.reshape(stretch // LANES, LANES))))


def solution(mesh):
    rows = P(("blk", "uly"), None)
    return jax.shard_map(
        functools.partial(shards, mesh.shape["uly"], mesh.shape["blk"]),
        mesh=mesh,
        in_specs=(rows, rows, rows, P("blk")),
        out_specs=rows,
        check_vma=False,
    )
```

```python
import functools
import math

import jax
import jax.numpy as jnp
from jax import lax
from jax.experimental import pallas as pl
from jax.experimental.pallas import tpu as pltpu
from jax.sharding import PartitionSpec as P

HEAD_DIM = 128
LANES = 128
MESH = pl.DeviceIdType.MESH
LAST_DIMS = (((1,), (1,)), ((), ()))
SCALE = math.log2(math.e) / math.sqrt(HEAD_DIM)
Q, K, V = 0, 1, 2


def kernel(
    peers, stretches, rows, heads,
    queries, keys, values, doc_start, attended,
    q_buf, k_buf, v_buf, o_buf, doc_buf, oldest, scores, doc_sem,
    in_send, in_recv, halo_send, halo_recv, out_send, out_recv,
):
    stretch = peers * rows
    middle = peers // 2
    window = stretch // 2
    span = window + rows
    blk, me = lax.axis_index("blk"), lax.axis_index("uly")
    after, before = lax.rem(blk + 1, stretches), lax.rem(blk + stretches - 1, stretches)

    def peer(i):
        half = (i + 1) // 2
        return lax.rem(me + jnp.where(i % 2 == 1, half, peers - half), peers)

    def served(i):
        return jnp.where(i < middle, i, peers - 1 - i + middle)

    def token_rows(p, shift=0):
        return pl.ds(pl.multiple_of(p * rows + shift, rows), rows)

    def head_columns(p, head):
        return pl.ds(pl.multiple_of((p * heads + head) * HEAD_DIM, HEAD_DIM), HEAD_DIM)

    fetch = pltpu.make_async_copy(doc_start, doc_buf, doc_sem)
    fetch.start()

    barrier = pltpu.get_barrier_semaphore()

    def greet(i, carry):
        pl.semaphore_signal(barrier, inc=1, device_id=(blk, peer(i)), device_id_type=MESH)
        return carry

    lax.fori_loop(1, peers, greet, 0)
    pl.semaphore_signal(barrier, inc=1, device_id=(before, me), device_id_type=MESH)
    pl.semaphore_wait(barrier, peers)

    operands = {Q: (queries, q_buf, 0), K: (keys, k_buf, window), V: (values, v_buf, window)}
    order = (K, V, Q)

    def inbound(head, t, src_peer, dst_peer):
        source, buffer, shift = operands[t]
        return pltpu.make_async_remote_copy(
            src_ref=source.at[:, head_columns(dst_peer, head)],
            dst_ref=buffer.at[head, token_rows(src_peer, shift)],
            send_sem=in_send.at[head, t, dst_peer],
            recv_sem=in_recv.at[head, t, src_peer],
            device_id=(blk, dst_peer),
            device_id_type=MESH,
        )

    def own(head, t):
        source, buffer, shift = operands[t]
        return pltpu.make_async_copy(
            source.at[:, head_columns(me, head)],
            buffer.at[head, token_rows(me, shift)],
            in_recv.at[head, t, me],
        )

    for head in range(heads):
        for t in order:
            own(head, t).start()

            def send(i, carry):
                p = peer(i)
                inbound(head, t, me, p).start()
                return carry

            lax.fori_loop(1, peers, send, 0)

    fetch.wait()
    for group in range(stretch // LANES):
        starts = jnp.transpose(jnp.broadcast_to(doc_buf[group : group + 1, :], (LANES, LANES)))
        token = group * LANES + lax.broadcasted_iota(jnp.int32, (LANES, LANES), 0)
        oldest[group * LANES : (group + 1) * LANES, :] = jnp.maximum(
            starts - blk * stretch + window, token + 1
        )

    def arrived(head, t, low, high):
        def wait(p, carry):
            inbound(head, t, p, me).wait_recv()
            return carry

        lax.fori_loop(low, high, wait, 0)

    def halo(head, t):
        buffer = operands[t][1]
        return pltpu.make_async_remote_copy(
            src_ref=buffer.at[head, pl.ds(stretch, window)],
            dst_ref=buffer.at[head, pl.ds(0, window)],
            send_sem=halo_send.at[head, t],
            recv_sem=halo_recv.at[head, t],
            device_id=(after, me),
            device_id_type=MESH,
        )

    def outbound(head, src_peer, dst_peer):
        return pltpu.make_async_remote_copy(
            src_ref=o_buf.at[head, token_rows(dst_peer)],
            dst_ref=attended.at[:, head_columns(src_peer, head)],
            send_sem=out_send.at[head, dst_peer],
            recv_sem=out_recv.at[head, src_peer],
            device_id=(blk, dst_peer),
            device_id_type=MESH,
        )

    def own_out(head):
        return pltpu.make_async_copy(
            o_buf.at[head, token_rows(me)],
            attended.at[:, head_columns(me, head)],
            out_recv.at[head, me],
        )

    def send_out(head, p):
        @pl.when(p == me)
        def _():
            own_out(head).start()

        @pl.when(p != me)
        def _():
            outbound(head, me, p).start()

    def attend(head, p):
        first = p * rows

        def key_rows(c):
            return pl.ds(pl.multiple_of(first + c * rows, rows), rows)

        query = q_buf[head, token_rows(p)]
        low = oldest[token_rows(p)] - first
        lane = lax.broadcasted_iota(jnp.int32, (rows, LANES), 1)
        row = lax.broadcasted_iota(jnp.int32, (rows, LANES), 0)
        top = jnp.full((rows, LANES), -jnp.inf, jnp.float32)
        for c in range(span // rows):
            tile = lax.dot_general(
                query, k_buf[head, key_rows(c)], LAST_DIMS, preferred_element_type=jnp.float32
            )
            for at in range(c * rows, (c + 1) * rows, LANES):
                allowed = lane + at >= low
                if at >= window:
                    allowed = allowed & (lane <= row - (at - window))
                part = jnp.where(allowed, tile[:, at - c * rows : at - c * rows + LANES], -jnp.inf)
                top = jnp.maximum(top, part)
                scores[:, at : at + LANES] = part
        row_max = jnp.broadcast_to(jnp.max(top, axis=1, keepdims=True) * SCALE, (rows, LANES))
        mixed = jnp.zeros((rows, HEAD_DIM), jnp.float32)
        total = jnp.zeros((rows, LANES), jnp.float32)
        for c in range(span // rows):
            weights = []
            for at in range(c * rows, (c + 1) * rows, LANES):
                probs = jnp.exp2(scores[:, at : at + LANES] * SCALE - row_max)
                total = total + probs
                weights.append(probs.astype(jnp.bfloat16))
            mixed = mixed + jnp.dot(
                jnp.concatenate(weights, axis=1),
                v_buf[head, key_rows(c)],
                preferred_element_type=jnp.float32,
            )
        mixed = mixed / jnp.sum(total, axis=1, keepdims=True)
        o_buf[head, token_rows(p)] = mixed.astype(jnp.bfloat16)

    for head in range(heads):
        for t in (K, V):
            arrived(head, t, middle, peers)
            halo(head, t).start()
        for t in (K, V):
            arrived(head, t, 0, middle)
        for t in (K, V):
            halo(head, t).wait_recv()

        def block(i, carry):
            p = served(i)
            inbound(head, Q, p, me).wait_recv()
            attend(head, p)
            send_out(head, p)
            return carry

        lax.fori_loop(0, peers, block, 0)

    for head in range(heads):
        for t in (K, V):
            halo(head, t).wait_send()

        def settle(i, carry):
            p = peer(i)
            for t in order:
                inbound(head, t, me, p).wait_send()
            outbound(head, p, p).wait_recv()
            outbound(head, me, p).wait_send()
            return carry

        lax.fori_loop(1, peers, settle, 0)
        own_out(head).wait()


def shards(peers, stretches, queries, keys, values, doc_start):
    rows, width = queries.shape
    stretch = rows * peers
    window = stretch // 2
    heads = width // peers // HEAD_DIM
    operands = (queries, keys, values, doc_start.reshape(stretch // LANES, LANES))
    return pl.pallas_call(
        functools.partial(kernel, peers, stretches, rows, heads),
        out_shape=jax.ShapeDtypeStruct((rows, width), jnp.bfloat16),
        in_specs=[pl.BlockSpec(memory_space=pltpu.HBM)] * 4,
        out_specs=pl.BlockSpec(memory_space=pl.ANY),
        scratch_shapes=[
            pltpu.VMEM((heads, stretch, HEAD_DIM), jnp.bfloat16),
            pltpu.VMEM((heads, stretch + window, HEAD_DIM), jnp.bfloat16),
            pltpu.VMEM((heads, stretch + window, HEAD_DIM), jnp.bfloat16),
            pltpu.VMEM((heads, stretch, HEAD_DIM), jnp.bfloat16),
            pltpu.VMEM((stretch // LANES, LANES), jnp.int32),
            pltpu.VMEM((stretch, LANES), jnp.int32),
            pltpu.VMEM((rows, window + rows), jnp.float32),
            pltpu.SemaphoreType.DMA,
            pltpu.SemaphoreType.DMA((heads, 3, peers)),
            pltpu.SemaphoreType.DMA((heads, 3, peers)),
            pltpu.SemaphoreType.DMA((heads, 3)),
            pltpu.SemaphoreType.DMA((heads, 3)),
            pltpu.SemaphoreType.DMA((heads, peers)),
            pltpu.SemaphoreType.DMA((heads, peers)),
        ],
        compiler_params=pltpu.CompilerParams(
            collective_id=0, has_side_effects=True, vmem_limit_bytes=48 << 20
        ),
    )(*(pltpu.with_memory_space_constraint(operand, pltpu.HBM) for operand in operands))


def solution(mesh):
    rows = P(("blk", "uly"), None)
    return jax.shard_map(
        functools.partial(shards, mesh.shape["uly"], mesh.shape["blk"]),
        mesh=mesh,
        in_specs=(rows, rows, rows, P("blk")),
        out_specs=rows,
        check_vma=False,
    )
```

```python
import functools
import math

import jax
import jax.numpy as jnp
from jax import lax
from jax.experimental import pallas as pl
from jax.experimental.pallas import tpu as pltpu
from jax.sharding import PartitionSpec as P

HEAD_DIM = 128
LANES = 128
MESH = pl.DeviceIdType.MESH
LAST_DIMS = (((1,), (1,)), ((), ()))
SCALE = math.log2(math.e) / math.sqrt(HEAD_DIM)
Q, K, V = 0, 1, 2


def kernel(
    peers, stretches, rows, heads,
    queries, keys, values, doc_start, attended,
    q_buf, k_buf, v_buf, o_buf, doc_buf, oldest, scores, doc_sem,
    in_send, in_recv, halo_send, halo_recv, out_send, out_recv, out_own,
):
    stretch = peers * rows
    middle = peers // 2
    window = stretch // 2
    span = window + rows
    blk, me = lax.axis_index("blk"), lax.axis_index("uly")
    after, before = lax.rem(blk + 1, stretches), lax.rem(blk + stretches - 1, stretches)

    def peer(i):
        half = (i + 1) // 2
        return lax.rem(me + jnp.where(i % 2 == 1, half, peers - half), peers)

    def served(i):
        return jnp.where(i < middle, i, peers - 1 - i + middle)

    def token_rows(p, shift=0):
        return pl.ds(pl.multiple_of(p * rows + shift, rows), rows)

    def head_columns(p, head):
        return pl.ds(pl.multiple_of((p * heads + head) * HEAD_DIM, HEAD_DIM), HEAD_DIM)

    fetch = pltpu.make_async_copy(doc_start, doc_buf, doc_sem)
    fetch.start()

    barrier = pltpu.get_barrier_semaphore()

    def greet(i, carry):
        pl.semaphore_signal(barrier, inc=1, device_id=(blk, peer(i)), device_id_type=MESH)
        return carry

    lax.fori_loop(1, peers, greet, 0)
    pl.semaphore_signal(barrier, inc=1, device_id=(before, me), device_id_type=MESH)
    pl.semaphore_wait(barrier, peers)

    operands = {Q: (queries, q_buf, 0), K: (keys, k_buf, window), V: (values, v_buf, window)}
    order = (K, V, Q)

    def inbound(head, t, src_peer, dst_peer):
        source, buffer, shift = operands[t]
        return pltpu.make_async_remote_copy(
            src_ref=source.at[:, head_columns(dst_peer, head)],
            dst_ref=buffer.at[head, token_rows(src_peer, shift)],
            send_sem=in_send.at[t],
            recv_sem=in_recv.at[head, t, src_peer],
            device_id=(blk, dst_peer),
            device_id_type=MESH,
        )

    def own(head, t):
        source, buffer, shift = operands[t]
        return pltpu.make_async_copy(
            source.at[:, head_columns(me, head)],
            buffer.at[head, token_rows(me, shift)],
            in_recv.at[head, t, me],
        )

    for head in range(heads):
        for t in order:
            own(head, t).start()

            def send(i, carry):
                p = peer(i)
                inbound(head, t, me, p).start()
                return carry

            lax.fori_loop(1, peers, send, 0)

    fetch.wait()
    for group in range(stretch // LANES):
        starts = jnp.transpose(jnp.broadcast_to(doc_buf[group : group + 1, :], (LANES, LANES)))
        token = group * LANES + lax.broadcasted_iota(jnp.int32, (LANES, LANES), 0)
        oldest[group * LANES : (group + 1) * LANES, :] = jnp.maximum(
            starts - blk * stretch + window, token + 1
        )

    def arrived(head, t, low, high):
        def wait(p, carry):
            inbound(head, t, p, me).wait_recv()
            return carry

        lax.fori_loop(low, high, wait, 0)

    def halo(head, t):
        buffer = operands[t][1]
        return pltpu.make_async_remote_copy(
            src_ref=buffer.at[head, pl.ds(stretch, window)],
            dst_ref=buffer.at[head, pl.ds(0, window)],
            send_sem=halo_send.at[head, t],
            recv_sem=halo_recv.at[head, t],
            device_id=(after, me),
            device_id_type=MESH,
        )

    def outbound(head, src_peer, dst_peer):
        return pltpu.make_async_remote_copy(
            src_ref=o_buf.at[head, token_rows(dst_peer)],
            dst_ref=attended.at[:, head_columns(src_peer, head)],
            send_sem=out_send,
            recv_sem=out_recv,
            device_id=(blk, dst_peer),
            device_id_type=MESH,
        )

    def own_out(head):
        return pltpu.make_async_copy(
            o_buf.at[head, token_rows(me)],
            attended.at[:, head_columns(me, head)],
            out_own.at[head],
        )

    def send_out(head, p):
        @pl.when(p == me)
        def _():
            own_out(head).start()

        @pl.when(p != me)
        def _():
            outbound(head, me, p).start()

    def attend(head, p):
        first = p * rows

        def key_rows(c):
            return pl.ds(pl.multiple_of(first + c * rows, rows), rows)

        query = q_buf[head, token_rows(p)]
        low = oldest[token_rows(p)] - first
        lane = lax.broadcasted_iota(jnp.int32, (rows, LANES), 1)
        row = lax.broadcasted_iota(jnp.int32, (rows, LANES), 0)
        top = jnp.full((rows, LANES), -jnp.inf, jnp.float32)
        for c in range(span // rows):
            tile = lax.dot_general(
                query, k_buf[head, key_rows(c)], LAST_DIMS, preferred_element_type=jnp.float32
            )
            for at in range(c * rows, (c + 1) * rows, LANES):
                allowed = lane + at >= low
                if at >= window:
                    allowed = allowed & (lane <= row - (at - window))
                part = jnp.where(allowed, tile[:, at - c * rows : at - c * rows + LANES], -jnp.inf)
                top = jnp.maximum(top, part)
                scores[:, at : at + LANES] = part
        row_max = jnp.broadcast_to(jnp.max(top, axis=1, keepdims=True) * SCALE, (rows, LANES))
        mixed = jnp.zeros((rows, HEAD_DIM), jnp.float32)
        total = jnp.zeros((rows, LANES), jnp.float32)
        for c in range(span // rows):
            weights = []
            for at in range(c * rows, (c + 1) * rows, LANES):
                probs = jnp.exp2(scores[:, at : at + LANES] * SCALE - row_max)
                total = total + probs
                weights.append(probs.astype(jnp.bfloat16))
            mixed = mixed + jnp.dot(
                jnp.concatenate(weights, axis=1),
                v_buf[head, key_rows(c)],
                preferred_element_type=jnp.float32,
            )
        mixed = mixed / jnp.sum(total, axis=1, keepdims=True)
        o_buf[head, token_rows(p)] = mixed.astype(jnp.bfloat16)

    for head in range(heads):
        for t in (K, V):
            arrived(head, t, middle, peers)
            halo(head, t).start()
        for t in (K, V):
            arrived(head, t, 0, middle)
        for t in (K, V):
            halo(head, t).wait_recv()

        def block(i, carry):
            p = served(i)
            inbound(head, Q, p, me).wait_recv()
            attend(head, p)
            send_out(head, p)
            return carry

        lax.fori_loop(0, peers, block, 0)

    def remote_columns(send_sem):
        columns = pl.ds(0, (peers - 1) * heads * HEAD_DIM)
        return pltpu.make_async_remote_copy(
            src_ref=queries.at[:, columns],
            dst_ref=attended.at[:, columns],
            send_sem=send_sem,
            recv_sem=out_recv,
            device_id=(after, me),
            device_id_type=MESH,
        )

    for head in range(heads):
        for t in (K, V):
            halo(head, t).wait_send()
        own_out(head).wait()
    for t in order:
        remote_columns(in_send.at[t]).wait_send()
    remote_columns(out_send).wait_send()
    remote_columns(out_send).wait_recv()


def shards(peers, stretches, queries, keys, values, doc_start):
    rows, width = queries.shape
    stretch = rows * peers
    window = stretch // 2
    heads = width // peers // HEAD_DIM
    operands = (queries, keys, values, doc_start.reshape(stretch // LANES, LANES))
    return pl.pallas_call(
        functools.partial(kernel, peers, stretches, rows, heads),
        out_shape=jax.ShapeDtypeStruct((rows, width), jnp.bfloat16),
        in_specs=[pl.BlockSpec(memory_space=pltpu.HBM)] * 4,
        out_specs=pl.BlockSpec(memory_space=pl.ANY),
        scratch_shapes=[
            pltpu.VMEM((heads, stretch, HEAD_DIM), jnp.bfloat16),
            pltpu.VMEM((heads, stretch + window, HEAD_DIM), jnp.bfloat16),
            pltpu.VMEM((heads, stretch + window, HEAD_DIM), jnp.bfloat16),
            pltpu.VMEM((heads, stretch, HEAD_DIM), jnp.bfloat16),
            pltpu.VMEM((stretch // LANES, LANES), jnp.int32),
            pltpu.VMEM((stretch, LANES), jnp.int32),
            pltpu.VMEM((rows, window + rows), jnp.float32),
            pltpu.SemaphoreType.DMA,
            pltpu.SemaphoreType.DMA((3,)),
            pltpu.SemaphoreType.DMA((heads, 3, peers)),
            pltpu.SemaphoreType.DMA((heads, 3)),
            pltpu.SemaphoreType.DMA((heads, 3)),
            pltpu.SemaphoreType.DMA,
            pltpu.SemaphoreType.DMA,
            pltpu.SemaphoreType.DMA((heads,)),
        ],
        compiler_params=pltpu.CompilerParams(
            collective_id=0, has_side_effects=True, vmem_limit_bytes=48 << 20
        ),
    )(*(pltpu.with_memory_space_constraint(operand, pltpu.HBM) for operand in operands))


def solution(mesh):
    rows = P(("blk", "uly"), None)
    return jax.shard_map(
        functools.partial(shards, mesh.shape["uly"], mesh.shape["blk"]),
        mesh=mesh,
        in_specs=(rows, rows, rows, P("blk")),
        out_specs=rows,
        check_vma=False,
    )
```

```python
import functools
import math

import jax
import jax.numpy as jnp
from jax import lax
from jax.experimental import pallas as pl
from jax.experimental.pallas import tpu as pltpu
from jax.sharding import PartitionSpec as P

HEAD_DIM = 128
LANES = 128
MESH = pl.DeviceIdType.MESH
LAST_DIMS = (((1,), (1,)), ((), ()))
SCALE = math.log2(math.e) / math.sqrt(HEAD_DIM)
Q, K, V = 0, 1, 2


def kernel(
    peers, stretches, rows, heads,
    queries, keys, values, doc_start, attended,
    q_buf, k_buf, v_buf, o_buf, doc_buf, oldest, scores, doc_sem,
    in_send, in_recv, halo_send, halo_recv, out_send, out_recv, out_own,
):
    stretch = peers * rows
    middle = peers // 2
    window = stretch // 2
    span = window + rows
    blk, me = lax.axis_index("blk"), lax.axis_index("uly")
    after, before = lax.rem(blk + 1, stretches), lax.rem(blk + stretches - 1, stretches)

    def peer(i):
        half = (i + 1) // 2
        return lax.rem(me + jnp.where(i % 2 == 1, half, peers - half), peers)

    def served(i):
        places = sum(jnp.where(i // 2 == k, 2 * z, 0) for k, z in enumerate((0, 1, 2, 3, 6, 7, 5, 4)))
        return places + i % 2

    def token_rows(p, shift=0):
        return pl.ds(pl.multiple_of(p * rows + shift, rows), rows)

    def head_columns(p, head):
        return pl.ds(pl.multiple_of((p * heads + head) * HEAD_DIM, HEAD_DIM), HEAD_DIM)

    barrier = pltpu.get_barrier_semaphore()

    def greet(i, carry):
        pl.semaphore_signal(barrier, inc=1, device_id=(blk, peer(i)), device_id_type=MESH)
        return carry

    lax.fori_loop(1, peers, greet, 0)
    pl.semaphore_signal(barrier, inc=1, device_id=(before, me), device_id_type=MESH)
    pl.semaphore_wait(barrier, peers)

    operands = {Q: (queries, q_buf, 0), K: (keys, k_buf, window), V: (values, v_buf, window)}
    order = (K, V, Q)

    def inbound(head, t, src_peer, dst_peer):
        source, buffer, shift = operands[t]
        return pltpu.make_async_remote_copy(
            src_ref=source.at[:, head_columns(dst_peer, head)],
            dst_ref=buffer.at[head, token_rows(src_peer, shift)],
            send_sem=in_send.at[t],
            recv_sem=in_recv.at[head, t, src_peer],
            device_id=(blk, dst_peer),
            device_id_type=MESH,
        )

    def own(head, t):
        source, buffer, shift = operands[t]
        return pltpu.make_async_copy(
            source.at[:, head_columns(me, head)],
            buffer.at[head, token_rows(me, shift)],
            in_recv.at[head, t, me],
        )

    for head in range(heads):
        for t in order:

            def send(i, carry):
                p = peer(i)
                inbound(head, t, me, p).start()
                return carry

            lax.fori_loop(1, peers, send, 0)
            own(head, t).start()

    fetch = pltpu.make_async_copy(doc_start, doc_buf, doc_sem)
    fetch.start()
    fetch.wait()
    for group in range(stretch // LANES):
        starts = jnp.transpose(jnp.broadcast_to(doc_buf[group : group + 1, :], (LANES, LANES)))
        token = group * LANES + lax.broadcasted_iota(jnp.int32, (LANES, LANES), 0)
        oldest[group * LANES : (group + 1) * LANES, :] = jnp.maximum(
            starts - blk * stretch + window, token + 1
        )

    def arrived(head, t, low, high):
        def wait(p, carry):
            inbound(head, t, p, me).wait_recv()
            return carry

        lax.fori_loop(low, high, wait, 0)

    def halo(head, t):
        buffer = operands[t][1]
        return pltpu.make_async_remote_copy(
            src_ref=buffer.at[head, pl.ds(stretch, window)],
            dst_ref=buffer.at[head, pl.ds(0, window)],
            send_sem=halo_send.at[head, t],
            recv_sem=halo_recv.at[head, t],
            device_id=(after, me),
            device_id_type=MESH,
        )

    def outbound(head, src_peer, dst_peer):
        return pltpu.make_async_remote_copy(
            src_ref=o_buf.at[head, token_rows(dst_peer)],
            dst_ref=attended.at[:, head_columns(src_peer, head)],
            send_sem=out_send,
            recv_sem=out_recv,
            device_id=(blk, dst_peer),
            device_id_type=MESH,
        )

    def own_out(head):
        return pltpu.make_async_copy(
            o_buf.at[head, token_rows(me)],
            attended.at[:, head_columns(me, head)],
            out_own.at[head],
        )

    def send_out(head, p):
        @pl.when(p == me)
        def _():
            own_out(head).start()

        @pl.when(p != me)
        def _():
            outbound(head, me, p).start()

    def attend(head, p):
        first = p * rows

        def key_rows(c):
            return pl.ds(pl.multiple_of(first + c * rows, rows), rows)

        query = q_buf[head, token_rows(p)]
        low = oldest[token_rows(p)] - first
        lane = lax.broadcasted_iota(jnp.int32, (rows, LANES), 1)
        row = lax.broadcasted_iota(jnp.int32, (rows, LANES), 0)
        top = jnp.full((rows, LANES), -jnp.inf, jnp.float32)
        for c in range(span // rows):
            tile = lax.dot_general(
                query, k_buf[head, key_rows(c)], LAST_DIMS, preferred_element_type=jnp.float32
            )
            for at in range(c * rows, (c + 1) * rows, LANES):
                allowed = lane + at >= low
                if at >= window:
                    allowed = allowed & (lane <= row - (at - window))
                part = jnp.where(allowed, tile[:, at - c * rows : at - c * rows + LANES], -jnp.inf)
                top = jnp.maximum(top, part)
                scores[:, at : at + LANES] = part
        row_max = jnp.broadcast_to(jnp.max(top, axis=1, keepdims=True) * SCALE, (rows, LANES))
        mixed = jnp.zeros((rows, HEAD_DIM), jnp.float32)
        total = jnp.zeros((rows, LANES), jnp.float32)
        for c in range(span // rows):
            weights = []
            for at in range(c * rows, (c + 1) * rows, LANES):
                probs = jnp.exp2(scores[:, at : at + LANES] * SCALE - row_max)
                total = total + probs
                weights.append(probs.astype(jnp.bfloat16))
            mixed = mixed + jnp.dot(
                jnp.concatenate(weights, axis=1),
                v_buf[head, key_rows(c)],
                preferred_element_type=jnp.float32,
            )
        mixed = mixed / jnp.sum(total, axis=1, keepdims=True)
        o_buf[head, token_rows(p)] = mixed.astype(jnp.bfloat16)

    for head in range(heads):
        for t in (K, V):
            arrived(head, t, middle, peers)
            halo(head, t).start()
        for t in (K, V):
            arrived(head, t, 0, middle)
        for t in (K, V):
            halo(head, t).wait_recv()

        def block(i, carry):
            p = served(i)
            inbound(head, Q, p, me).wait_recv()
            attend(head, p)
            send_out(head, p)
            return carry

        lax.fori_loop(0, peers, block, 0)

    def remote_columns(send_sem):
        columns = pl.ds(0, (peers - 1) * heads * HEAD_DIM)
        return pltpu.make_async_remote_copy(
            src_ref=queries.at[:, columns],
            dst_ref=attended.at[:, columns],
            send_sem=send_sem,
            recv_sem=out_recv,
            device_id=(after, me),
            device_id_type=MESH,
        )

    for head in range(heads):
        for t in (K, V):
            halo(head, t).wait_send()
        own_out(head).wait()
    for t in order:
        remote_columns(in_send.at[t]).wait_send()
    remote_columns(out_send).wait_send()
    remote_columns(out_send).wait_recv()


def shards(peers, stretches, queries, keys, values, doc_start):
    rows, width = queries.shape
    stretch = rows * peers
    window = stretch // 2
    heads = width // peers // HEAD_DIM
    operands = (queries, keys, values, doc_start.reshape(stretch // LANES, LANES))
    return pl.pallas_call(
        functools.partial(kernel, peers, stretches, rows, heads),
        out_shape=jax.ShapeDtypeStruct((rows, width), jnp.bfloat16),
        in_specs=[pl.BlockSpec(memory_space=pltpu.HBM)] * 4,
        out_specs=pl.BlockSpec(memory_space=pl.ANY),
        scratch_shapes=[
            pltpu.VMEM((heads, stretch, HEAD_DIM), jnp.bfloat16),
            pltpu.VMEM((heads, stretch + window, HEAD_DIM), jnp.bfloat16),
            pltpu.VMEM((heads, stretch + window, HEAD_DIM), jnp.bfloat16),
            pltpu.VMEM((heads, stretch, HEAD_DIM), jnp.bfloat16),
            pltpu.VMEM((stretch // LANES, LANES), jnp.int32),
            pltpu.VMEM((stretch, LANES), jnp.int32),
            pltpu.VMEM((rows, window + rows), jnp.float32),
            pltpu.SemaphoreType.DMA,
            pltpu.SemaphoreType.DMA((3,)),
            pltpu.SemaphoreType.DMA((heads, 3, peers)),
            pltpu.SemaphoreType.DMA((heads, 3)),
            pltpu.SemaphoreType.DMA((heads, 3)),
            pltpu.SemaphoreType.DMA,
            pltpu.SemaphoreType.DMA,
            pltpu.SemaphoreType.DMA((heads,)),
        ],
        compiler_params=pltpu.CompilerParams(
            collective_id=0, has_side_effects=True, vmem_limit_bytes=48 << 20
        ),
    )(*(pltpu.with_memory_space_constraint(operand, pltpu.HBM) for operand in operands))


def solution(mesh):
    rows = P(("blk", "uly"), None)
    return jax.shard_map(
        functools.partial(shards, mesh.shape["uly"], mesh.shape["blk"]),
        mesh=mesh,
        in_specs=(rows, rows, rows, P("blk")),
        out_specs=rows,
        check_vma=False,
    )
```

```python
import functools
import math

import jax
import jax.numpy as jnp
from jax import lax
from jax.experimental import pallas as pl
from jax.experimental.pallas import tpu as pltpu
from jax.sharding import PartitionSpec as P

HEAD_DIM = 128
LANES = 128
MESH = pl.DeviceIdType.MESH
LAST_DIMS = (((1,), (1,)), ((), ()))
SCALE = math.log2(math.e) / math.sqrt(HEAD_DIM)
Q, K, V = 0, 1, 2


def kernel(
    peers, stretches, rows, heads,
    queries, keys, values, doc_start, attended,
    q_buf, k_buf, v_buf, o_buf, doc_buf, oldest, scores, doc_sem,
    in_send, in_recv, halo_send, halo_recv, out_send, out_recv, out_own,
):
    stretch = peers * rows
    middle = peers // 2
    window = stretch // 2
    span = window + rows
    blk, me = lax.axis_index("blk"), lax.axis_index("uly")
    after, before = lax.rem(blk + 1, stretches), lax.rem(blk + stretches - 1, stretches)

    def peer(i):
        half = (i + 1) // 2
        return lax.rem(me + jnp.where(i % 2 == 1, half, peers - half), peers)

    def served(i):
        places = sum(jnp.where(i // 2 == k, 2 * z, 0) for k, z in enumerate((0, 1, 2, 3, 6, 7, 5, 4)))
        return places + i % 2

    def token_rows(p, shift=0):
        return pl.ds(pl.multiple_of(p * rows + shift, rows), rows)

    def head_columns(p, head):
        return pl.ds(pl.multiple_of((p * heads + head) * HEAD_DIM, HEAD_DIM), HEAD_DIM)

    fetch = pltpu.make_async_copy(doc_start, doc_buf, doc_sem)
    fetch.start()

    barrier = pltpu.get_barrier_semaphore()

    def greet(i, carry):
        pl.semaphore_signal(barrier, inc=1, device_id=(blk, peer(i)), device_id_type=MESH)
        return carry

    lax.fori_loop(1, peers, greet, 0)
    pl.semaphore_signal(barrier, inc=1, device_id=(before, me), device_id_type=MESH)
    pl.semaphore_wait(barrier, peers)

    operands = {Q: (queries, q_buf, 0), K: (keys, k_buf, window), V: (values, v_buf, window)}
    order = (K, V, Q)

    def inbound(head, t, src_peer, dst_peer):
        source, buffer, shift = operands[t]
        return pltpu.make_async_remote_copy(
            src_ref=source.at[:, head_columns(dst_peer, head)],
            dst_ref=buffer.at[head, token_rows(src_peer, shift)],
            send_sem=in_send.at[t],
            recv_sem=in_recv.at[head, t, src_peer],
            device_id=(blk, dst_peer),
            device_id_type=MESH,
        )

    def own(head, t):
        source, buffer, shift = operands[t]
        return pltpu.make_async_copy(
            source.at[:, head_columns(me, head)],
            buffer.at[head, token_rows(me, shift)],
            in_recv.at[head, t, me],
        )

    for head in range(heads):
        for t in order:
            own(head, t).start()

            def send(i, carry):
                p = peer(i)
                inbound(head, t, me, p).start()
                return carry

            lax.fori_loop(1, peers, send, 0)

    fetch.wait()
    for group in range(stretch // LANES):
        starts = jnp.transpose(jnp.broadcast_to(doc_buf[group : group + 1, :], (LANES, LANES)))
        token = group * LANES + lax.broadcasted_iota(jnp.int32, (LANES, LANES), 0)
        oldest[group * LANES : (group + 1) * LANES, :] = jnp.maximum(
            starts - blk * stretch + window, token + 1
        )

    def arrived(head, t, low, high):
        def wait(p, carry):
            inbound(head, t, p, me).wait_recv()
            return carry

        lax.fori_loop(low, high, wait, 0)

    def halo(head, t):
        buffer = operands[t][1]
        return pltpu.make_async_remote_copy(
            src_ref=buffer.at[head, pl.ds(stretch, window)],
            dst_ref=buffer.at[head, pl.ds(0, window)],
            send_sem=halo_send.at[head, t],
            recv_sem=halo_recv.at[head, t],
            device_id=(after, me),
            device_id_type=MESH,
        )

    def outbound(head, src_peer, dst_peer):
        return pltpu.make_async_remote_copy(
            src_ref=o_buf.at[head, token_rows(dst_peer)],
            dst_ref=attended.at[:, head_columns(src_peer, head)],
            send_sem=out_send,
            recv_sem=out_recv,
            device_id=(blk, dst_peer),
            device_id_type=MESH,
        )

    def own_out(head):
        return pltpu.make_async_copy(
            o_buf.at[head, token_rows(me)],
            attended.at[:, head_columns(me, head)],
            out_own.at[head],
        )

    def send_out(head, p):
        @pl.when(p == me)
        def _():
            own_out(head).start()

        @pl.when(p != me)
        def _():
            outbound(head, me, p).start()

    def attend(head, p):
        first = p * rows

        def key_rows(c):
            return pl.ds(pl.multiple_of(first + c * rows, rows), rows)

        query = q_buf[head, token_rows(p)]
        low = oldest[token_rows(p)] - first
        lane = lax.broadcasted_iota(jnp.int32, (rows, LANES), 1)
        row = lax.broadcasted_iota(jnp.int32, (rows, LANES), 0)
        top = jnp.full((rows, LANES), -jnp.inf, jnp.float32)
        for c in range(span // rows):
            tile = lax.dot_general(
                query, k_buf[head, key_rows(c)], LAST_DIMS, preferred_element_type=jnp.float32
            )
            for at in range(c * rows, (c + 1) * rows, LANES):
                allowed = lane + at >= low
                if at >= window:
                    allowed = allowed & (lane <= row - (at - window))
                part = jnp.where(allowed, tile[:, at - c * rows : at - c * rows + LANES], -jnp.inf)
                top = jnp.maximum(top, part)
                scores[:, at : at + LANES] = part
        row_max = jnp.broadcast_to(jnp.max(top, axis=1, keepdims=True) * SCALE, (rows, LANES))
        mixed = jnp.zeros((rows, HEAD_DIM), jnp.float32)
        total = jnp.zeros((rows, LANES), jnp.float32)
        for c in range(span // rows):
            weights = []
            for at in range(c * rows, (c + 1) * rows, LANES):
                probs = jnp.exp2(scores[:, at : at + LANES] * SCALE - row_max)
                total = total + probs
                weights.append(probs.astype(jnp.bfloat16))
            mixed = mixed + jnp.dot(
                jnp.concatenate(weights, axis=1),
                v_buf[head, key_rows(c)],
                preferred_element_type=jnp.float32,
            )
        mixed = mixed / jnp.sum(total, axis=1, keepdims=True)
        o_buf[head, token_rows(p)] = mixed.astype(jnp.bfloat16)

    for head in range(heads):
        for t in (K, V):
            arrived(head, t, middle, peers)
            halo(head, t).start()
        for t in (K, V):
            arrived(head, t, 0, middle)
        for t in (K, V):
            halo(head, t).wait_recv()

        def block(i, carry):
            p = served(i)
            inbound(head, Q, p, me).wait_recv()
            attend(head, p)
            send_out(head, p)
            return carry

        lax.fori_loop(0, peers, block, 0)

    def remote_columns(send_sem):
        columns = pl.ds(0, (peers - 1) * heads * HEAD_DIM)
        return pltpu.make_async_remote_copy(
            src_ref=queries.at[:, columns],
            dst_ref=attended.at[:, columns],
            send_sem=send_sem,
            recv_sem=out_recv,
            device_id=(after, me),
            device_id_type=MESH,
        )

    for head in range(heads):
        for t in (K, V):
            halo(head, t).wait_send()
        own_out(head).wait()
    for t in order:
        remote_columns(in_send.at[t]).wait_send()
    remote_columns(out_send).wait_send()
    remote_columns(out_send).wait_recv()


def shards(peers, stretches, queries, keys, values, doc_start):
    rows, width = queries.shape
    stretch = rows * peers
    window = stretch // 2
    heads = width // peers // HEAD_DIM
    operands = (queries, keys, values, doc_start.reshape(stretch // LANES, LANES))
    return pl.pallas_call(
        functools.partial(kernel, peers, stretches, rows, heads),
        out_shape=jax.ShapeDtypeStruct((rows, width), jnp.bfloat16),
        in_specs=[pl.BlockSpec(memory_space=pltpu.HBM)] * 4,
        out_specs=pl.BlockSpec(memory_space=pl.ANY),
        scratch_shapes=[
            pltpu.VMEM((heads, stretch, HEAD_DIM), jnp.bfloat16),
            pltpu.VMEM((heads, stretch + window, HEAD_DIM), jnp.bfloat16),
            pltpu.VMEM((heads, stretch + window, HEAD_DIM), jnp.bfloat16),
            pltpu.VMEM((heads, stretch, HEAD_DIM), jnp.bfloat16),
            pltpu.VMEM((stretch // LANES, LANES), jnp.int32),
            pltpu.VMEM((stretch, LANES), jnp.int32),
            pltpu.VMEM((rows, window + rows), jnp.float32),
            pltpu.SemaphoreType.DMA,
            pltpu.SemaphoreType.DMA((3,)),
            pltpu.SemaphoreType.DMA((heads, 3, peers)),
            pltpu.SemaphoreType.DMA((heads, 3)),
            pltpu.SemaphoreType.DMA((heads, 3)),
            pltpu.SemaphoreType.DMA,
            pltpu.SemaphoreType.DMA,
            pltpu.SemaphoreType.DMA((heads,)),
        ],
        compiler_params=pltpu.CompilerParams(
            collective_id=0, has_side_effects=True, vmem_limit_bytes=48 << 20
        ),
    )(*(pltpu.with_memory_space_constraint(operand, pltpu.HBM) for operand in operands))


def solution(mesh):
    rows = P(("blk", "uly"), None)
    return jax.shard_map(
        functools.partial(shards, mesh.shape["uly"], mesh.shape["blk"]),
        mesh=mesh,
        in_specs=(rows, rows, rows, P("blk")),
        out_specs=rows,
        check_vma=False,
    )
```
